32 devices in a mesh: row: 4 (over y, x), col: 8 (over z, core).
Axes of the slice: x: 2, y: 2, z: 4, core: 2. Of those that a mesh axis runs over, the one named last changes fastest.
Arguments:
- boundary_start: float32 [16384, 128], P('row'), may hold values from -6 to 6
- volume_start: float32 [256, 512, 128], P(('row', 'col')), may hold values from -6 to 6
- diag_part: float32 [16384], P(('row', 'col')), may hold values from 1 to 2
- incident: float32 [16384, 128], P(('row', 'col')), may hold values from -6 to 6
- kernel: float32 [16384, 16384], P('row', 'col'), may hold values from -0.015625 to 0.015625
- elem_mats: float32 [256, 512, 512], P(('row', 'col')), may hold values from -0.078125 to 0.078125
- trace_owner: int32 [16384, 1], replicated, may hold values from 0 to 31; in each aligned block of 512 rows (0 to 511, 512 to 1023, ...) at most 32 rows name the same one
- trace_slot: int32 [16384], replicated, may hold values from 0 to 4095
- return_owner: int32 [16384, 1], replicated, may hold values from 0 to 31; in each aligned block of 512 rows (0 to 511, 512 to 1023, ...) at most 32 rows name the same one
- return_slot: int32 [16384], replicated, may hold values from 0 to 4095
- face_match: int32 [256, 64], P(('row', 'col')), may hold values from 0 to 63, each once within a row
Outputs:
- boundary_final: float32 [16384, 128], P('row')
- volume_final: float32 [256, 512, 128], P(('row', 'col'))
The draws below stay inside these ranges and needn't reach their ends.
Inputs may be any that keep to these rules, and one draw needn't show every extreme that they name: `trace_owner`: in each aligned block of 512 boundary rows (the rows of one device), no device is named more than 32 times; some device is named exactly 32 times in some block. `return_owner`: in each aligned block of 512 boundary rows (the rows of one device), no device is named more than 32 times; some device is named exactly 32 times in some block. `face_match`: each row is a permutation of 0 to 63.
All inputs are finite; a program needn't handle non-finite values.
Results may differ from the reference program's by a relative error of at most 0.0001.
Values sent between devices are 32-bit elements; how exact they have to be, the bound alone decides.
A program may use at most 128 MiB of HBM per device.

```python
import math
import jax
import jax.numpy as jnp
import numpy as np
from jax import lax

NB = 16384
R = 128
NODES = 512
FACE = 64
E_DEV = 8
ITERS = 3
ELEMS = 256
RB = 512
CAP = 32
DEVICES = 32


def set_ends(entries, own_key, smallest, top_value):
    index_at = [jax.random.randint(jax.random.fold_in(own_key, axis), (), 0, length) for axis, length in enumerate(entries.shape)]
    widest = entries.shape.index(max(entries.shape))
    beside = index_at[:widest] + [(index_at[widest] + 1) % entries.shape[widest]] + index_at[widest + 1:]
    return entries.at[tuple(index_at)].set(smallest).at[tuple(beside)].set(top_value)


def shard_levels(rng, dims, shards, low, high):
    factor_of, own = 1.0, jax.random.fold_in(rng, 6)
    for position, blocks in shards:
        heights = jnp.exp(jax.random.uniform(jax.random.fold_in(own, position), (blocks,), jnp.float32, low / len(shards), high / len(shards)))
        factor_of = factor_of * jnp.repeat(heights, dims[position] // blocks).reshape([-1 if axis == position else 1 for axis in range(len(dims))])
    return factor_of


def shared_out(key, own, number, rows, number_of, top, most, slope):
    sequence = jax.random.permutation(key, number_of)
    crowded, ordinary = shares(number_of, rows * top, most, slope, True), shares(number_of, rows * top, most, slope, False)
    places = jnp.arange(number_of)

    def named(tallies, turn):
        used = int((tallies > 0).sum())
        fixed = max(1, used // 4)
        shifted = fixed + (places - fixed + turn * (used - fixed)) % max(1, number_of - fixed)
        return jnp.zeros((number_of,), jnp.int32).at[sequence[jnp.where(places < fixed, places, shifted)]].set(jnp.asarray(tallies, jnp.int32))

    tallies = jnp.where(number % 4 == 0, named(crowded, number // 4), named(ordinary, number - number // 4 - 1))
    mixed = jax.random.permutation(jax.random.fold_in(own, 3), number_of)
    giver, sink = mixed[0:number_of // 2 * 2:2], mixed[1:number_of // 2 * 2:2]
    slack = jnp.minimum(tallies[giver] - 1, most - tallies[sink]) // 2
    slack = jnp.where((giver == sequence[0]) | (sink == sequence[0]) | (tallies[sink] == 0), 0, jnp.maximum(slack, 0))
    shifted = jax.random.randint(jax.random.fold_in(own, 4), (number_of // 2,), 0, 1 << 20) % (slack + 1)
    tallies = tallies.at[giver].add(-shifted).at[sink].add(shifted)
    members = jnp.searchsorted(jnp.cumsum(tallies), jnp.arange(rows * top), side="right").astype(jnp.int32)
    grid = members.reshape(top, rows).T
    grid = grid[jax.random.permutation(jax.random.fold_in(own, 1), rows)]
    turn = jax.random.randint(jax.random.fold_in(own, 2), (rows, 1), 0, top)
    return jnp.take_along_axis(grid, (jnp.arange(top)[None, :] + turn) % top, axis=1)


def shares(count, total, bound, lean, full):
    portions = [(1 << 20) // math.isqrt(rank ** lean) + 1 for rank in range(1, count + 1)]
    largest = bound if full else min(bound, max(-(-total // count), total * portions[0] // sum(portions)))
    least = 1 if total - largest >= count - 1 else 0
    given, spare = [largest] + [least] * (count - 1), total - largest - least * (count - 1)
    while spare > 0:
        candidates = [i for i in range(1, count) if given[i] < largest] or [i for i in range(1, count) if given[i] < bound]
        whole, left = sum([portions[i] for i in candidates]), spare
        for i in candidates:
            more = min(bound - given[i], max(1, left * portions[i] // whole), spare)
            given[i] = given[i] + more
            spare = spare - more
    return np.array(given)


def scatter_about(rng, dims, spread, bound, split=(), kind=jnp.bfloat16):
    values = spread * jax.random.normal(rng, dims, jnp.float32)
    if split:
        values = values * shard_levels(rng, dims, split, -0.22, 0.18)
    return jnp.clip(values, -bound, bound).astype(kind)


def setup_inputs(seed: int = 0) -> dict:
    splits = jax.random.split(jax.random.key(seed), 12)
    boundary_start = scatter_about(splits[0], (NB, R), 1.0, 6.0, ((0, 4),), jnp.float32)
    volume_start = scatter_about(splits[1], (ELEMS, NODES, R), 1.0, 6.0, ((0, 32),), jnp.float32)
    diag_part = jnp.clip(jnp.exp(math.log(2.0) - 0.6931472 * jax.random.uniform(splits[2], (NB,), jnp.float32) ** shard_levels(splits[2], (NB,), ((0, 32),), -0.2, 0.2)), 1.0, 2.0)
    incident = scatter_about(splits[3], (NB, R), 1.0, 6.0, ((0, 32),), jnp.float32)
    kernel = scatter_about(splits[4], (NB, NB), (8 * NB) ** -0.5, 0.015625, ((0, 4), (1, 8)), jnp.float32)
    elem_mats = scatter_about(splits[5], (ELEMS, NODES, NODES), (11 * NODES) ** -0.5, 0.078125, ((0, 32),), jnp.float32)
    trace_owner_keys = jax.random.split(jax.random.fold_in(splits[6], 1), NB // RB)
    trace_owner_turns = jax.random.permutation(jax.random.fold_in(splits[6], 3), NB // RB)
    trace_owner = jax.vmap(lambda own, number: shared_out(jax.random.fold_in(splits[6], 2), own, number, RB, DEVICES, 1, CAP, 1))(trace_owner_keys, trace_owner_turns).reshape((NB, 1))
    trace_slot = set_ends(jax.random.randint(splits[7], (NB,), 0, E_DEV * NODES), jax.random.fold_in(splits[7], 1), 0, (E_DEV * NODES) - 1).astype(jnp.int32)
    return_owner_keys = jax.random.split(jax.random.fold_in(splits[8], 1), NB // RB)
    return_owner_turns = jax.random.permutation(jax.random.fold_in(splits[8], 3), NB // RB)
    return_owner = jax.vmap(lambda own, number: shared_out(jax.random.fold_in(splits[8], 2), own, number, RB, DEVICES, 1, CAP, 2))(return_owner_keys, return_owner_turns).reshape((NB, 1))
    return_slot = set_ends(jax.random.randint(splits[9], (NB,), 0, E_DEV * NODES), jax.random.fold_in(splits[9], 1), 0, (E_DEV * NODES) - 1).astype(jnp.int32)
    face_match = jax.vmap(lambda own: jax.random.permutation(own, FACE))(jax.random.split(splits[10], ELEMS)).reshape((ELEMS, FACE)).astype(jnp.int32)
    return {"boundary_start": boundary_start, "volume_start": volume_start, "diag_part": diag_part, "incident": incident, "kernel": kernel, "elem_mats": elem_mats, "trace_owner": trace_owner, "trace_slot": trace_slot, "return_owner": return_owner, "return_slot": return_slot, "face_match": face_match}


boundary_step = 0.5
volume_step = 0.6
face_weight = 0.5


def reference(boundary_start, volume_start, diag_part, incident, kernel, elem_mats, trace_owner, trace_slot, return_owner, return_slot, face_match):
    highest = lax.Precision.HIGHEST
    owner_nodes = E_DEV * NODES
    trace_index = (trace_owner[:, 0] * owner_nodes + trace_slot).astype(jnp.int32)
    return_index = (return_owner[:, 0] * owner_nodes + return_slot).astype(jnp.int32)
    boundary = boundary_start
    volume = volume_start
    for sweep_index in range(ITERS):
        volume_flat = volume.reshape(ELEMS * NODES, R)
        traced = volume_flat[trace_index]
        image = jnp.dot(kernel, boundary, precision=highest, preferred_element_type=jnp.float32)
        residual = diag_part[:, None] * boundary + image - incident - traced
        flux_field = jnp.zeros_like(volume_flat).at[return_index].add(boundary).reshape(ELEMS, NODES, R)
        lower_faces = jnp.concatenate([jnp.zeros((E_DEV, FACE, R), jnp.float32), volume[:ELEMS - E_DEV, NODES - FACE:, :]], axis=0)
        matched = jax.vmap(lambda face_rows, face_order: face_rows[face_order])(lower_faces, face_match)
        applied = jnp.einsum("enm,emr->enr", elem_mats, volume, precision=highest)
        updated = volume - volume_step * (volume + applied - flux_field)
        volume = updated.at[:, :FACE, :].add(volume_step * face_weight * matched)
        boundary = boundary - boundary_step * residual
    return boundary, volume
```

```python
import functools

import jax
import jax.numpy as jnp
from jax import lax
from jax.experimental import pallas as pl
from jax.experimental.pallas import tpu as pltpu
from jax.sharding import PartitionSpec as P

ITERS = 3


boundary_step = 0.5
volume_step = 0.6
face_weight = 0.5


def parts(block):
    high = block.astype(jnp.bfloat16)
    low = (block - high.astype(jnp.float32)).astype(jnp.bfloat16)
    return high, low


def wide_of(block):
    return jnp.concatenate(parts(block), axis=1)


def product(left, right):
    return jnp.dot(left, right, preferred_element_type=jnp.float32)


def one_hot(hits):
    return jnp.where(hits, 1.0, 0.0).astype(jnp.bfloat16)


def sweeps_kernel(*refs):
    boundary_start, volume_start, kernel, elem_mats, diag, incident = refs[:6]
    trace_send, trace_take, flux_send, flux_take, face_rows = refs[6:11]
    volume, out = refs[11:13]
    (
        kernel_held, elem_held, share, panels, panel_wide, partial, from_pair, from_line,
        flux_leaving, flux_landed, flux_wide, trace_leaving, trace_landed, trace_wide, faces,
    ) = refs[13:28]
    (
        kernel_sem, elem_sem, volume_sem, share_sem, move_send, move_recv, row_send, row_recv,
        pair_send, pair_recv, line_send, line_recv, flux_out, flux_in, trace_out, trace_in,
        face_out, face_in, out_sem, final_send, final_recv, back_send, back_recv,
    ) = refs[28:]

    rows_n, cols_n = lax.axis_size("row"), lax.axis_size("col")
    pairs = cols_n // 2
    per_panel = cols_n // rows_n
    r, c = lax.axis_index("row"), lax.axis_index("col")
    z, h = c // 2, c % 2
    partner = z * 2 + (1 - h)
    target_row, target_col = c % rows_n, r * per_panel + c // rows_n
    source_row, source_col = c // per_panel, (c % per_panel) * rows_n + r
    stays = (target_row == r) & (target_col == c)
    moves = jnp.logical_not(stays)
    device = r * cols_n + c
    has_next, has_prev = device < rows_n * cols_n - 1, device > 0
    next_row, next_col = (device + 1) // cols_n, (device + 1) % cols_n

    share_rows, columns = share.shape
    elem_count, node_count = elem_held.shape[:2]
    face_count = faces.shape[2]
    capacity = flux_leaving.shape[2]
    slots = flux_wide.shape[0]
    above = pairs - 1 - z

    def target(k):
        return jnp.where(k < above, pairs - 1 - k, k - above)

    def block_of(i):
        t = target(i // 2)
        return t * 2 + jnp.where(i % 2 == 0, 1 - h, h)

    def load(i):
        b = block_of(i)
        return pltpu.make_async_copy(
            kernel.at[pl.ds(pl.multiple_of(b * share_rows, share_rows), share_rows), :],
            kernel_held.at[b], kernel_sem.at[i],
        )

    share_load = pltpu.make_async_copy(
        boundary_start.at[pl.ds(pl.multiple_of(c * share_rows, share_rows), share_rows), :], share, share_sem
    )
    volume_load = pltpu.make_async_copy(volume_start, volume, volume_sem)
    elem_load = pltpu.make_async_copy(elem_mats, elem_held, elem_sem)
    share_load.start()
    volume_load.start()
    for i in range(cols_n):
        load(i).start()
    elem_load.start()

    barrier = pltpu.get_barrier_semaphore()

    def greet(row, col):
        pl.semaphore_signal(barrier, inc=1, device_id=(row, col), device_id_type=pl.DeviceIdType.MESH)

    for step in range(1, cols_n):
        greet(r, (c + step) % cols_n)
    for step in range(1, rows_n):
        greet((r + step) % rows_n, c)

    @pl.when(moves)
    def _():
        greet(source_row, source_col)

    @pl.when((c == 0) & (r > 0))
    def _():
        greet(r - 1, cols_n - 1)

    greeted = cols_n - 1 + rows_n - 1 + jnp.where(stays, 0, 1)
    greeted += jnp.where((c == cols_n - 1) & (r < rows_n - 1), 1, 0)
    pl.semaphore_wait(barrier, greeted)

    def remote(src, dst, send, recv, row, col):
        return pltpu.make_async_remote_copy(
            src_ref=src, dst_ref=dst, send_sem=send, recv_sem=recv,
            device_id=(row, col), device_id_type=pl.DeviceIdType.MESH,
        )

    def move(par):
        return remote(
            share, panels.at[par, target_row], move_send, move_recv.at[par], target_row, target_col
        )

    def row_copy(par, step):
        piece = panels.at[par, r]
        return remote(
            piece, piece, row_send.at[step - 1], row_recv.at[par, step - 1], (r + step) % rows_n, c
        )

    def pair_copy(par, t):
        return remote(
            partial.at[t * 2 + (1 - h)], from_pair.at[par, t], pair_send.at[t], pair_recv.at[par, t], r, partner
        )

    def up_copy(par, t):
        return remote(
            partial.at[t * 2 + h], from_line.at[par, t + 1],
            line_send.at[t + 1], line_recv.at[par, t + 1], r, c + 2,
        )

    def down_copy(par, t):
        return remote(
            partial.at[t * 2 + h], from_line.at[par, t], line_send.at[t], line_recv.at[par, t], r, c - 2
        )

    def flux_copy(par, piece, step):
        member = (c + step) % cols_n
        return remote(
            flux_leaving.at[piece, member], flux_landed.at[par, c, piece],
            flux_out.at[piece, step - 1], flux_in.at[par, piece, step - 1], r, member,
        )

    def trace_copy(par, step):
        row = (r + step) % rows_n
        return remote(
            trace_leaving.at[row], trace_landed.at[par, r], trace_out.at[step - 1],
            trace_in.at[par, step - 1], row, c,
        )

    def face_copy(par, e):
        start = pl.multiple_of(e * node_count + (node_count - face_count), 8)
        return remote(
            volume.at[pl.ds(start, face_count), :], faces.at[par, e],
            face_out.at[e], face_in.at[par, e], next_row, next_col,
        )

    def send_faces(par):
        @pl.when(has_next)
        def _():
            for e in range(elem_count):
                face_copy(par, e).start()

    def wait_faces_sent(par):
        @pl.when(has_next)
        def _():
            for e in range(elem_count):
                face_copy(par, e).wait_send()

    def send_traces(par):
        def pick(row, k, carry):
            for p in range(capacity):
                slot = trace_send[(row * cols_n + k) * capacity + p]
                trace_leaving[row, k, pl.ds(p, 1), :] = volume[pl.ds(slot, 1), :]
            return carry

        for step in range(1, rows_n):
            lax.fori_loop(0, cols_n, functools.partial(pick, (r + step) % rows_n), 0)
            trace_copy(par, step).start()
        lax.fori_loop(0, cols_n, functools.partial(pick, r), 0)
        trace_landed[par, r] = trace_leaving[r]

    def wait_traces_sent(par):
        for step in range(1, rows_n):
            trace_copy(par, step).wait_send()

    def relay_up(par, t):
        up_copy(par, t).start()

    def relay_down(par, t):
        down_copy(par, t).start()

    def take_piece(par, step, carry):
        piece = (r + rows_n - step) % rows_n

        @pl.when(step > 0)
        def _():
            row_copy(par, jnp.maximum(step, 1)).wait_recv()

        wide = wide_of(panels[par, piece])
        panel_wide[pl.ds(pl.multiple_of(piece * share_rows, share_rows), share_rows), :] = wide
        place = lax.broadcasted_iota(jnp.int32, (cols_n * capacity, share_rows), 1)
        picked = product(one_hot(place == flux_send[piece]), wide)
        picked = picked[:, :columns] + picked[:, columns:]
        flux_leaving[piece] = picked.reshape(cols_n, capacity, columns)
        for other in range(1, cols_n):
            flux_copy(par, piece, other).start()
        flux_landed[par, c, piece] = flux_leaving[piece, c]
        return carry

    def product_step(s, par, i, carry):
        b = block_of(i)
        t = target(i // 2)

        @pl.when(s == 0)
        def _():
            load(i).wait()

        high, low = parts(kernel_held[b])
        place = lax.broadcasted_iota(jnp.int32, (share_rows, trace_wide.shape[1]), 0)
        wide = product(high, panel_wide[...]) + product(low, panel_wide[...])
        wide -= product(one_hot(place == trace_take[b]), trace_wide[b])
        partial[b] = wide[:, :columns] + wide[:, columns:]

        @pl.when(i % 2 == 0)
        def _():
            pair_copy(par, t).start()

        @pl.when(i % 2 == 1)
        def _():
            pair_copy(par, t).wait_recv()
            partial[b] += from_pair[par, t]

            @pl.when((z == 0) & (t > z))
            def _():
                up_copy(par, t).start()

            @pl.when((z == pairs - 1) & (t < z))
            def _():
                down_copy(par, t).start()

        return carry

    def volume_step_of(par, e, carry):
        nodes = pl.ds(pl.multiple_of(e * node_count, node_count), node_count)
        field = volume[nodes, :]
        high, low = parts(elem_held[e])
        field_wide = wide_of(field)
        wide = product(high, field_wide) + product(low, field_wide)
        place = lax.broadcasted_iota(jnp.int32, (node_count, slots), 0) + e * node_count
        wide -= product(one_hot(place == flux_take[...]), flux_wide[...])
        volume[nodes, :] = field - volume_step * (field + wide[:, :columns] + wide[:, columns:])
        node = lax.broadcasted_iota(jnp.int32, (face_count, face_count), 1)
        face = product(one_hot(node == face_rows[e]), wide_of(faces[par, e]))
        matched = face[:, :columns] + face[:, columns:]
        lower = pl.ds(pl.multiple_of(e * node_count, node_count), face_count)
        volume[lower, :] += volume_step * face_weight * matched
        return carry

    gaps = max(1, pairs - 2)
    chunk = -(-elem_count // gaps)

    def relay_step(par, stage, carry):
        @pl.when((z >= 1) & (z <= stage) & (stage <= pairs - 2))
        def _():
            t = pairs - 1 + z - stage
            up_copy(par, t - 0).wait_recv()
            partial[t * 2 + h] += from_line[par, t + 1]
            up_copy(par, t).start()

        @pl.when((z <= pairs - 2) & (above <= stage) & (stage <= pairs - 2))
        def _():
            t = stage - above
            down_copy(par, t).wait_recv()
            partial[t * 2 + h] += from_line[par, t]
            down_copy(par, t).start()

        first = jnp.minimum((stage - 1) * chunk, elem_count)
        last = jnp.minimum(stage * chunk, elem_count)
        lax.fori_loop(first, last, functools.partial(volume_step_of, par), 0)
        return carry

    def sweep(s, carry):
        par = s % 2
        lax.fori_loop(0, rows_n, functools.partial(take_piece, par), 0)

        for step in range(1, rows_n):
            trace_copy(par, step).wait_recv()
        for b in range(cols_n):
            landed = trace_landed[par, :, b].reshape(rows_n * capacity, columns)
            trace_wide[b] = wide_of(landed)

        lax.fori_loop(0, cols_n, functools.partial(product_step, s, par), 0)

        @pl.when(s == 0)
        def _():
            elem_load.wait()

        for piece in range(rows_n):
            for other in range(1, cols_n):
                flux_copy(par, piece, other).wait_recv()
        flux_wide[...] = wide_of(flux_landed[par].reshape(slots, columns))

        @pl.when(has_prev)
        def _():
            for e in range(elem_count):
                face_copy(par, e).wait_recv()

        wait_faces_sent(par)
        wait_traces_sent(par)
        lax.fori_loop(1, 1 + gaps, functools.partial(relay_step, par), 0)

        @pl.when(s < ITERS - 1)
        def _():
            send_faces(1 - par)
            send_traces(1 - par)

        own = z * 2 + h

        @pl.when(z > 0)
        def _():
            up_copy(par, z).wait_recv()
            partial[own] += from_line[par, z + 1]

        @pl.when(z < pairs - 1)
        def _():
            down_copy(par, z).wait_recv()
            partial[own] += from_line[par, z]

        @pl.when(moves)
        def _():
            move(par).wait_send()

        held = share[...]
        middle = held - boundary_step * (diag[...] * held - incident[...])
        share[...] = middle - boundary_step * partial[own]

        @pl.when((s < ITERS - 1) & moves)
        def _():
            move(1 - par).start()

        for step in range(1, rows_n):
            row_copy(par, step).wait_send()
        for t in range(pairs):
            pair_copy(par, t).wait_send()

            @pl.when(t > z)
            def _():
                up_copy(par, t).wait_send()

            @pl.when(t < z)
            def _():
                down_copy(par, t).wait_send()

        for piece in range(rows_n):
            for other in range(1, cols_n):
                flux_copy(par, piece, other).wait_send()

        @pl.when(s < ITERS - 1)
        def _():
            finish_spread(1 - par)

        return carry

    def finish_spread(par):
        @pl.when(stays)
        def _():
            panels[par, r] = share[...]

        @pl.when(moves)
        def _():
            move(par).wait_recv()

        for step in range(1, rows_n):
            row_copy(par, step).start()

    share_load.wait()

    @pl.when(moves)
    def _():
        move(0).start()

    @pl.when(jnp.logical_not(has_prev))
    def _():
        faces[...] = jnp.zeros_like(faces)

    volume_load.wait()
    send_faces(0)
    send_traces(0)
    finish_spread(0)
    lax.fori_loop(0, ITERS, sweep, 0)

    keep = pltpu.make_async_copy(share, out.at[c], out_sem)
    keep.start()

    def final_up(src, origin, step):
        return remote(
            src, out.at[origin], final_send.at[0, step - 1], final_recv.at[0, step - 1], r, c + 2
        )

    def final_down(src, origin, step):
        return remote(
            src, out.at[origin], final_send.at[1, step - 1], final_recv.at[1, step - 1], r, c - 2
        )

    def back(src, origin, place):
        return remote(src, out.at[origin], back_send.at[place], back_recv.at[place], r, partner)

    @pl.when(z < pairs - 1)
    def _():
        final_up(share, c, 1).start()

    @pl.when(z > 0)
    def _():
        final_down(share, c, 1).start()

    back(share, c, z).start()
    for step in range(1, pairs):
        lower, upper = c - 2 * step, c + 2 * step

        @pl.when(z >= step)
        def _():
            final_up(share, lower, step).wait_recv()

            @pl.when(z < pairs - 1)
            def _():
                final_up(out.at[lower], lower, step + 1).start()

            back(out.at[lower], lower, z - step).start()

        @pl.when(z + step < pairs)
        def _():
            final_down(share, upper, step).wait_recv()

            @pl.when(z > 0)
            def _():
                final_down(out.at[upper], upper, step + 1).start()

            back(out.at[upper], upper, z + step).start()

    keep.wait()
    for place in range(pairs):
        back(share, c, place).wait_recv()
    for place in range(pairs):
        back(share, c, place).wait_send()
    for step in range(1, pairs + 1):
        @pl.when((z < pairs - 1) & (z >= step - 1))
        def _():
            final_up(share, c, step).wait_send()

        @pl.when((z > 0) & (z + step - 1 < pairs))
        def _():
            final_down(share, c, step).wait_send()


def sweeps(boundary_start, volume_flat, kernel, elem_mats, diag, incident, plans, capacity, face_rows):
    rows_n, cols_n = lax.axis_size("row"), lax.axis_size("col")
    pairs = cols_n // 2
    share_rows, columns = incident.shape
    panel_rows = kernel.shape[1]
    elem_count, face_count = face_rows.shape[:2]
    block = (share_rows, columns)
    slots = rows_n * cols_n * capacity
    f32, bf16 = jnp.float32, jnp.bfloat16
    in_vmem, anywhere = pl.BlockSpec(memory_space=pltpu.VMEM), pl.BlockSpec(memory_space=pl.ANY)
    in_smem = pl.BlockSpec(memory_space=pltpu.SMEM)
    dma = pltpu.SemaphoreType.DMA
    scratch = [
        pltpu.VMEM((cols_n, share_rows, panel_rows), f32),
        pltpu.VMEM(elem_mats.shape, f32),
        pltpu.VMEM(block, f32),
        pltpu.VMEM((2, rows_n) + block, f32),
        pltpu.VMEM((panel_rows, 2 * columns), bf16),
        pltpu.VMEM((cols_n,) + block, f32),
        pltpu.VMEM((2, pairs) + block, f32),
        pltpu.VMEM((2, pairs + 1) + block, f32),
        pltpu.VMEM((rows_n, cols_n, capacity, columns), f32),
        pltpu.VMEM((2, cols_n, rows_n, capacity, columns), f32),
        pltpu.VMEM((slots, 2 * columns), bf16),
        pltpu.VMEM((rows_n, cols_n, capacity, columns), f32),
        pltpu.VMEM((2, rows_n, cols_n, capacity, columns), f32),
        pltpu.VMEM((cols_n, rows_n * capacity, 2 * columns), bf16),
        pltpu.VMEM((2, elem_count, face_count, columns), f32),
        dma((cols_n,)), dma, dma, dma,
        dma, dma((2,)), dma((rows_n - 1,)), dma((2, rows_n - 1)),
        dma((pairs,)), dma((2, pairs)), dma((pairs + 1,)), dma((2, pairs + 1)),
        dma((rows_n, cols_n - 1)), dma((2, rows_n, cols_n - 1)),
        dma((rows_n - 1,)), dma((2, rows_n - 1)),
        dma((elem_count,)), dma((2, elem_count)),
        dma, dma((2, pairs)), dma((2, pairs)), dma((pairs,)), dma((pairs,)),
    ]
    return pl.pallas_call(
        sweeps_kernel,
        out_shape=[
            jax.ShapeDtypeStruct(volume_flat.shape, f32),
            jax.ShapeDtypeStruct((cols_n,) + block, f32),
        ],
        in_specs=[anywhere] * 4 + [in_vmem] * 2 + [in_smem] + [in_vmem] * 4,
        out_specs=[in_vmem, anywhere],
        scratch_shapes=scratch,
        compiler_params=pltpu.CompilerParams(
            collective_id=0, has_side_effects=True, vmem_limit_bytes=67043328
        ),
        cost_estimate=pl.CostEstimate(flops=1000, bytes_accessed=150_000_000, transcendentals=0),
    )(boundary_start, volume_flat, kernel, elem_mats, diag, incident, *plans, face_rows)


def shards(
    boundary_start,
    volume_start,
    diag_part,
    incident,
    kernel,
    elem_mats,
    trace_owner,
    trace_slot,
    return_owner,
    return_slot,
    face_match,
):
    rows_n, cols_n = lax.axis_size("row"), lax.axis_size("col")
    devices = rows_n * cols_n
    r, c = lax.axis_index("row"), lax.axis_index("col")
    device = r * cols_n + c
    share_rows = trace_slot.shape[0] // devices
    capacity = max(2, 2 * share_rows // devices)
    elem_count, node_count, columns = volume_start.shape

    trace_blocks = trace_owner[:, 0].reshape(devices, share_rows)
    trace_slots = trace_slot.reshape(devices, share_rows)
    return_blocks = return_owner[:, 0].reshape(devices, share_rows)
    return_slots = return_slot.reshape(devices, share_rows)
    own_trace = lax.dynamic_slice_in_dim(trace_blocks, r * cols_n, cols_n, 0)
    own_return = lax.dynamic_slice_in_dim(return_blocks, c * rows_n, rows_n, 0)
    row_owners = jnp.arange(rows_n, dtype=jnp.int32) * cols_n + c
    col_owners = r * cols_n + jnp.arange(cols_n, dtype=jnp.int32)
    masks = jnp.concatenate([
        trace_blocks == device,
        (own_trace[:, None, :] == row_owners[None, :, None]).reshape(devices, share_rows),
        (own_return[:, None, :] == col_owners[None, :, None]).reshape(devices, share_rows),
        return_blocks == device,
    ])
    places = jnp.broadcast_to(jnp.arange(share_rows, dtype=jnp.int32)[None, :], (2 * devices, share_rows))
    values = jnp.concatenate([trace_slots, places, return_slots]) + 1
    earlier = jnp.triu(jnp.ones((share_rows, share_rows), jnp.bfloat16))
    ranks = jnp.dot(masks.astype(jnp.bfloat16), earlier, preferred_element_type=jnp.float32)
    ranks = jnp.where(masks, ranks, 0.0)
    wanted = jnp.arange(1, capacity + 1, dtype=jnp.int32).astype(jnp.float32)
    hits = ranks[:, None, :] == wanted[None, :, None]
    plan = jnp.sum(jnp.where(hits, values[:, None, :], 0), axis=2) - 1
    plan = plan.reshape(4, devices * capacity)
    plans = (
        jnp.maximum(plan[0], 0),
        plan[1].reshape(cols_n, 1, rows_n * capacity),
        plan[2].reshape(rows_n, cols_n * capacity, 1),
        plan[3].reshape(1, devices * capacity),
    )
    volume_final, boundary_final = sweeps(
        boundary_start, volume_start.reshape(elem_count * node_count, columns), kernel, elem_mats,
        diag_part[:, None], incident, plans, capacity, face_match[:, :, None],
    )
    return (
        boundary_final.reshape(boundary_start.shape),
        volume_final.reshape(volume_start.shape),
    )


def solution(mesh):
    placed = (
        P("row", None),
        P(("row", "col"), None, None),
        P(("row", "col")),
        P(("row", "col"), None),
        P("row", "col"),
        P(("row", "col"), None, None),
        P(),
        P(),
        P(),
        P(),
        P(("row", "col"), None),
    )
    return jax.shard_map(
        shards,
        mesh=mesh,
        in_specs=placed,
        out_specs=(P("row", None), P(("row", "col"), None, None)),
        check_vma=False,
    )
```

```python
import functools

import jax
import jax.numpy as jnp
from jax import lax
from jax.experimental import pallas as pl
from jax.experimental.pallas import tpu as pltpu
from jax.sharding import PartitionSpec as P

ITERS = 3


boundary_step = 0.5
volume_step = 0.6
face_weight = 0.5


def parts(block):
    high = block.astype(jnp.bfloat16)
    low = (block - high.astype(jnp.float32)).astype(jnp.bfloat16)
    return high, low


def wide_of(block):
    return jnp.concatenate(parts(block), axis=1)


def product(left, right):
    return jnp.dot(left, right, preferred_element_type=jnp.float32)


def one_hot(hits):
    return jnp.where(hits, 1.0, 0.0).astype(jnp.bfloat16)


def sweeps_kernel(*refs):
    boundary_start, volume_start, kernel, elem_mats, diag_own, incident_own = refs[:6]
    trace_send, trace_take, flux_send, flux_take, face_rows = refs[6:11]
    volume, out = refs[11:13]
    (
        kernel_held, elem_held, diag_row, diag, incident, middle_out, middle, panels, panel_wide, partial, from_pair,
        from_row, from_line, flux_leaving, flux_landed, flux_wide, trace_leaving, trace_landed, trace_wide, faces,
    ) = refs[13:33]
    (
        kernel_sem, elem_sem, volume_sem, piece_sem, move_send, move_recv, start_send, start_recv, row_send, row_recv,
        pair_send, pair_recv, turn_send, turn_recv, line_send, line_recv, flux_out, flux_in, trace_out, trace_in,
        face_out, face_in, out_sem, final_send, final_recv, back_send, back_recv,
    ) = refs[33:]

    rows_n, cols_n = lax.axis_size("row"), lax.axis_size("col")
    pairs = cols_n // 2
    assert rows_n == pairs
    r, c = lax.axis_index("row"), lax.axis_index("col")
    z, h = c // 2, c % 2
    partner = z * 2 + (1 - h)
    target_row, target_col = c % rows_n, r * 2 + c // rows_n
    source_row, source_col = z, h * rows_n + r
    stays = (target_row == r) & (target_col == c)
    moves = jnp.logical_not(stays)
    device = r * cols_n + c
    has_next, has_prev = device < rows_n * cols_n - 1, device > 0
    next_row, next_col = (device + 1) // cols_n, (device + 1) % cols_n
    roots = r == z

    share_rows, columns = middle.shape
    elem_count, node_count = elem_held.shape[:2]
    face_count = faces.shape[2]
    capacity = flux_leaving.shape[2]
    slots = flux_wide.shape[0]
    above = pairs - 1 - z
    last_sweep = ITERS - 1

    def target(s, k):
        line = jnp.where(k < above, pairs - 1 - k, k - above)
        return jnp.where(s < last_sweep, (r + 1 + k) % rows_n, line)

    def block_of(s, t, side):
        return jnp.where(s < last_sweep, side * rows_n + t, t * 2 + side)

    def piece_of(step):
        return (r + rows_n - step) % rows_n

    def load(step, i):
        b, piece = block_of(0, target(0, i // 2), jnp.where(i % 2 == 0, 1 - h, h)), piece_of(step)
        return pltpu.make_async_copy(
            kernel.at[
                pl.ds(pl.multiple_of(b * share_rows, share_rows), share_rows),
                pl.ds(pl.multiple_of(piece * share_rows, share_rows), share_rows),
            ],
            kernel_held.at[b, piece], kernel_sem.at[step, i],
        )

    def start_rows(piece):
        return boundary_start.at[pl.ds(pl.multiple_of((h * rows_n + piece) * share_rows, share_rows), share_rows), :]

    def piece_load(piece):
        return pltpu.make_async_copy(start_rows(piece), panels.at[0, piece], piece_sem.at[piece])

    volume_load = pltpu.make_async_copy(volume_start, volume, volume_sem)
    elem_load = pltpu.make_async_copy(elem_mats, elem_held, elem_sem)

    @pl.when(roots)
    def _():
        for piece in range(rows_n):
            piece_load(piece).start()

    volume_load.start()
    for step in range(rows_n):
        for i in range(cols_n):
            load(step, i).start()
    elem_load.start()

    barrier = pltpu.get_barrier_semaphore()

    def greet(row, col):
        pl.semaphore_signal(barrier, inc=1, device_id=(row, col), device_id_type=pl.DeviceIdType.MESH)

    for step in range(1, cols_n):
        greet(r, (c + step) % cols_n)
    for step in range(1, rows_n):
        greet((r + step) % rows_n, c)

    @pl.when(moves)
    def _():
        greet(source_row, source_col)
        greet(target_row, target_col)

    @pl.when((c == 0) & (r > 0))
    def _():
        greet(r - 1, cols_n - 1)

    greeted = cols_n - 1 + rows_n - 1 + jnp.where(stays, 0, 2)
    greeted += jnp.where((c == cols_n - 1) & (r < rows_n - 1), 1, 0)
    pl.semaphore_wait(barrier, greeted)

    def remote(src, dst, send, recv, row, col):
        return pltpu.make_async_remote_copy(
            src_ref=src, dst_ref=dst, send_sem=send, recv_sem=recv,
            device_id=(row, col), device_id_type=pl.DeviceIdType.MESH,
        )

    def move_incident():
        return remote(incident_own, incident, move_send.at[0], move_recv.at[0], target_row, target_col)

    def move_diag():
        return remote(diag_own, diag_row, move_send.at[1], move_recv.at[1], target_row, target_col)

    def move_middle():
        return remote(middle_out, middle, move_send.at[2], move_recv.at[2], source_row, source_col)

    def start_copy(step):
        piece = (r + step) % rows_n
        return remote(
            start_rows(piece), panels.at[0, piece], start_send.at[step - 1], start_recv, piece, c
        )

    def row_copy(par, step):
        piece = panels.at[par, r]
        return remote(
            piece, piece, row_send.at[par, step - 1], row_recv.at[par, step - 1], (r + step) % rows_n, c
        )

    def row_sent(s, step):
        return (s > 0) | ((r + step) % rows_n != z)

    def pair_copy(par, s, t):
        return remote(
            partial.at[block_of(s, t, 1 - h)], from_pair.at[par, t], pair_send.at[t], pair_recv.at[par, t], r, partner
        )

    def turn_copy(par, t):
        return remote(
            partial.at[h * rows_n + t], from_row.at[par, r], turn_send.at[t], turn_recv.at[par, r], t, c
        )

    def turn_landed(par, t):
        return remote(
            partial.at[h * rows_n + t], from_row.at[par, t], turn_send.at[t], turn_recv.at[par, t], t, c
        )

    def up_copy(par, t):
        return remote(
            from_row.at[par, t], from_line.at[par, t + 1],
            line_send.at[t + 1], line_recv.at[par, t + 1], r, c + 2,
        )

    def down_copy(par, t):
        return remote(
            from_row.at[par, t], from_line.at[par, t], line_send.at[t], line_recv.at[par, t], r, c - 2
        )

    def flux_copy(par, piece, step):
        member = (c + step) % cols_n
        return remote(
            flux_leaving.at[piece, member], flux_landed.at[par, c, piece],
            flux_out.at[piece, step - 1], flux_in.at[par, piece, step - 1], r, member,
        )

    def trace_copy(par, step):
        row = (r + step) % rows_n
        return remote(
            trace_leaving.at[row], trace_landed.at[par, r], trace_out.at[step - 1],
            trace_in.at[par, step - 1], row, c,
        )

    def face_copy(par, e):
        start = pl.multiple_of(e * node_count + (node_count - face_count), 8)
        return remote(
            volume.at[pl.ds(start, face_count), :], faces.at[par, e],
            face_out.at[e], face_in.at[par, e], next_row, next_col,
        )

    def send_faces(par):
        @pl.when(has_next)
        def _():
            for e in range(elem_count):
                face_copy(par, e).start()

    def wait_faces_sent(par):
        @pl.when(has_next)
        def _():
            for e in range(elem_count):
                face_copy(par, e).wait_send()

    def send_traces(par):
        def pick(row, k, carry):
            for p in range(capacity):
                slot = trace_send[(row * cols_n + k) * capacity + p]
                trace_leaving[row, k, pl.ds(p, 1), :] = volume[pl.ds(slot, 1), :]
            return carry

        for step in range(1, rows_n):
            lax.fori_loop(0, cols_n, functools.partial(pick, (r + step) % rows_n), 0)
            trace_copy(par, step).start()
        lax.fori_loop(0, cols_n, functools.partial(pick, r), 0)
        trace_landed[par, r] = trace_leaving[r]

    def wait_traces_sent(par):
        for step in range(1, rows_n):
            trace_copy(par, step).wait_send()

    def take_piece(s, par, step, carry):
        piece = piece_of(step)
        last_step = step == rows_n - 1

        @pl.when((s == 0) & roots)
        def _():
            @pl.when(step > 0)
            def _():
                piece_load(piece).wait()

        @pl.when((step > 0) & ((s > 0) | jnp.logical_not(roots)))
        def _():
            row_copy(par, jnp.maximum(step, 1)).wait_recv()

        wide = wide_of(panels[par, piece])
        panel_wide[...] = wide
        place = lax.broadcasted_iota(jnp.int32, (share_rows, cols_n * capacity), 0)
        picked = lax.dot_general(
            one_hot(place == flux_send[piece]), wide, (((0,), (0,)), ((), ())), preferred_element_type=jnp.float32
        )
        picked = picked[:, :columns] + picked[:, columns:]
        flux_leaving[piece] = picked.reshape(cols_n, capacity, columns)
        for other in range(1, cols_n):
            flux_copy(par, piece, other).start()
        flux_landed[par, c, piece] = flux_leaving[piece, c]

        def product_step(i, carry):
            t = target(s, i // 2)
            theirs = i % 2 == 0
            b = block_of(s, t, jnp.where(theirs, 1 - h, h))

            @pl.when(s == 0)
            def _():
                load(step, i).wait()

            high, low = parts(kernel_held[b, piece])
            wide = product(high, panel_wide[...]) + product(low, panel_wide[...])
            partial[b] += wide[:, :columns] + wide[:, columns:]

            @pl.when(last_step & theirs)
            def _():
                pair_copy(par, s, t).start()

            @pl.when(last_step & jnp.logical_not(theirs))
            def _():
                pair_copy(par, s, t).wait_recv()
                stay = (s == last_sweep) | (t == r)

                @pl.when(stay)
                def _():
                    from_row[par, t] = partial[b] + from_pair[par, t]

                @pl.when(jnp.logical_not(stay))
                def _():
                    partial[b] += from_pair[par, t]
                    turn_copy(par, t).start()

            return carry

        return lax.fori_loop(0, cols_n, product_step, carry)

    def volume_step_of(par, e, carry):
        nodes = pl.ds(pl.multiple_of(e * node_count, node_count), node_count)
        field = volume[nodes, :]
        high, low = parts(elem_held[e])
        field_wide = wide_of(field)
        wide = product(high, field_wide) + product(low, field_wide)
        place = lax.broadcasted_iota(jnp.int32, (node_count, slots), 0) + e * node_count
        wide -= product(one_hot(place == flux_take[...]), flux_wide[...])
        volume[nodes, :] = field - volume_step * (field + wide[:, :columns] + wide[:, columns:])
        node = lax.broadcasted_iota(jnp.int32, (face_count, face_count), 0)
        face = lax.dot_general(
            one_hot(node == face_rows[e]), wide_of(faces[par, e]), (((0,), (0,)), ((), ())),
            preferred_element_type=jnp.float32,
        )
        matched = face[:, :columns] + face[:, columns:]
        lower = pl.ds(pl.multiple_of(e * node_count, node_count), face_count)
        volume[lower, :] += volume_step * face_weight * matched
        return carry

    gaps = pairs - 1
    chunk = -(-elem_count // gaps)

    def wait_turn(s, par, t):
        @pl.when((s < last_sweep) & (t != r))
        def _():
            turn_landed(par, t).wait_recv()

    def relay_step(s, par, stage, carry):
        @pl.when(z <= stage)
        def _():
            t = pairs - 1 + z - stage
            wait_turn(s, par, t)

            @pl.when(z > 0)
            def _():
                up_copy(par, t).wait_recv()
                from_row[par, t] += from_line[par, t + 1]

            up_copy(par, t).start()

        @pl.when(above <= stage)
        def _():
            t = stage - above
            wait_turn(s, par, t)

            @pl.when(above > 0)
            def _():
                down_copy(par, t).wait_recv()
                from_row[par, t] += from_line[par, t]

            down_copy(par, t).start()

        @pl.when(stage == 0)
        def _():
            @pl.when(s == 0)
            def _():
                elem_load.wait()

            for piece in range(rows_n):
                for other in range(1, cols_n):
                    flux_copy(par, piece, other).wait_recv()
            flux_wide[...] = wide_of(flux_landed[par].reshape(slots, columns))

            @pl.when(has_prev)
            def _():
                for e in range(elem_count):
                    face_copy(par, e).wait_recv()

            wait_faces_sent(par)
            wait_traces_sent(par)

        first = jnp.minimum(stage * chunk, elem_count)
        last = jnp.minimum((stage + 1) * chunk, elem_count)
        lax.fori_loop(first, last, functools.partial(volume_step_of, par), 0)
        return carry

    def take_trace(b, carry):
        place = lax.broadcasted_iota(jnp.int32, (share_rows, trace_wide.shape[1]), 0)
        wide = product(one_hot(place == trace_take[b]), trace_wide[b])
        partial[b] = -(wide[:, :columns] + wide[:, columns:])
        return carry

    def sweep(s, carry):
        par = s % 2
        for step in range(1, rows_n):
            trace_copy(par, step).wait_recv()
        for b in range(cols_n):
            landed = trace_landed[par, :, b].reshape(rows_n * capacity, columns)
            trace_wide[b] = wide_of(landed)
        lax.fori_loop(0, cols_n, take_trace, 0)

        def middle_of():
            held = panels[par, r]
            return held - boundary_step * (diag[...] * held - incident[...])

        @pl.when((s == last_sweep) & moves)
        def _():
            middle_out[...] = middle_of()
            move_middle().start()

        @pl.when((s == last_sweep) & stays)
        def _():
            middle[...] = middle_of()

        lax.fori_loop(0, rows_n, functools.partial(take_piece, s, par), 0)
        lax.fori_loop(0, gaps, functools.partial(relay_step, s, par), 0)

        @pl.when(s < last_sweep)
        def _():
            send_faces(1 - par)
            send_traces(1 - par)

        @pl.when((s == 0) & moves)
        def _():
            move_diag().wait_recv()
            move_incident().wait_recv()

        @pl.when(s == 0)
        def _():
            diag[...] = jnp.broadcast_to(diag_row[...], (columns, share_rows)).T

        @pl.when((s == last_sweep) & moves)
        def _():
            move_middle().wait_recv()

        wait_turn(s, par, z)

        @pl.when(z > 0)
        def _():
            up_copy(par, z).wait_recv()
            from_row[par, z] += from_line[par, z + 1]

        @pl.when(above > 0)
        def _():
            down_copy(par, z).wait_recv()
            from_row[par, z] += from_line[par, z]

        @pl.when(s == last_sweep)
        def _():
            panels[1 - par, r] = middle[...] - boundary_step * from_row[par, z]

        @pl.when(s < last_sweep)
        def _():
            panels[1 - par, r] = middle_of() - boundary_step * from_row[par, z]
            for step in range(1, rows_n):
                row_copy(1 - par, step).start()

        return carry

    def drain(s, par):
        for step in range(1, rows_n):
            @pl.when(row_sent(s, step))
            def _():
                row_copy(par, step).wait_send()

        for t in range(pairs):
            pair_copy(par, s, t).wait_send()

            @pl.when((s < last_sweep) & (t != r))
            def _():
                turn_copy(par, t).wait_send()

            @pl.when(t > z)
            def _():
                up_copy(par, t).wait_send()

            @pl.when(t < z)
            def _():
                down_copy(par, t).wait_send()

        for piece in range(rows_n):
            for other in range(1, cols_n):
                flux_copy(par, piece, other).wait_send()

    @pl.when(roots)
    def _():
        for step in range(1, rows_n):
            start_copy(step).start()

    @pl.when(moves)
    def _():
        move_diag().start()
        move_incident().start()

    @pl.when(stays)
    def _():
        diag_row[...] = diag_own[...]
        incident[...] = incident_own[...]

    @pl.when(jnp.logical_not(has_prev))
    def _():
        faces[...] = jnp.zeros_like(faces)

    volume_load.wait()
    send_faces(0)
    send_traces(0)

    @pl.when(roots)
    def _():
        piece_load(r).wait()

    @pl.when(jnp.logical_not(roots))
    def _():
        remote(start_rows(r), panels.at[0, r], start_send.at[0], start_recv, z, c).wait_recv()

    for step in range(1, rows_n):
        @pl.when(row_sent(0, step))
        def _():
            row_copy(0, step).start()

    def sweep_and_drain(s, carry):
        sweep(s, carry)
        drain(s, s % 2)
        return carry

    lax.fori_loop(0, ITERS, sweep_and_drain, 0)
    share = panels.at[ITERS % 2, r]

    keep = pltpu.make_async_copy(share, out.at[c], out_sem)
    keep.start()

    def final_up(src, origin, step):
        return remote(
            src, out.at[origin], final_send.at[0, step - 1], final_recv.at[0, step - 1], r, c + 2
        )

    def final_down(src, origin, step):
        return remote(
            src, out.at[origin], final_send.at[1, step - 1], final_recv.at[1, step - 1], r, c - 2
        )

    def back(src, origin, place):
        return remote(src, out.at[origin], back_send.at[place], back_recv.at[place], r, partner)

    @pl.when(z < pairs - 1)
    def _():
        final_up(share, c, 1).start()

    @pl.when(z > 0)
    def _():
        final_down(share, c, 1).start()

    back(share, c, z).start()
    for step in range(1, pairs):
        lower, upper = c - 2 * step, c + 2 * step

        @pl.when(z >= step)
        def _():
            final_up(share, lower, step).wait_recv()

            @pl.when(z < pairs - 1)
            def _():
                final_up(out.at[lower], lower, step + 1).start()

            back(out.at[lower], lower, z - step).start()

        @pl.when(z + step < pairs)
        def _():
            final_down(share, upper, step).wait_recv()

            @pl.when(z > 0)
            def _():
                final_down(out.at[upper], upper, step + 1).start()

            back(out.at[upper], upper, z + step).start()

    keep.wait()
    for place in range(pairs):
        back(share, c, place).wait_recv()
    for place in range(pairs):
        back(share, c, place).wait_send()
    for step in range(1, pairs + 1):
        @pl.when((z < pairs - 1) & (z >= step - 1))
        def _():
            final_up(share, c, step).wait_send()

        @pl.when((z > 0) & (z + step - 1 < pairs))
        def _():
            final_down(share, c, step).wait_send()

    @pl.when(roots)
    def _():
        for step in range(1, rows_n):
            start_copy(step).wait_send()

    @pl.when(moves)
    def _():
        move_diag().wait_send()
        move_incident().wait_send()
        move_middle().wait_send()


def sweeps(boundary_start, volume_flat, kernel, elem_mats, diag, incident, plans, capacity, face_rows):
    rows_n, cols_n = lax.axis_size("row"), lax.axis_size("col")
    pairs = cols_n // 2
    share_rows, columns = incident.shape
    elem_count, _, face_count = face_rows.shape
    block = (share_rows, columns)
    slots = rows_n * cols_n * capacity
    f32, bf16 = jnp.float32, jnp.bfloat16
    in_vmem, anywhere = pl.BlockSpec(memory_space=pltpu.VMEM), pl.BlockSpec(memory_space=pl.ANY)
    in_smem = pl.BlockSpec(memory_space=pltpu.SMEM)
    dma = pltpu.SemaphoreType.DMA
    scratch = [
        pltpu.VMEM((cols_n, rows_n, share_rows, share_rows), f32),
        pltpu.VMEM(elem_mats.shape, f32),
        pltpu.VMEM((1, share_rows), f32),
        pltpu.VMEM(block, f32),
        pltpu.VMEM(block, f32),
        pltpu.VMEM(block, f32),
        pltpu.VMEM(block, f32),
        pltpu.VMEM((2, rows_n) + block, f32),
        pltpu.VMEM((share_rows, 2 * columns), bf16),
        pltpu.VMEM((cols_n,) + block, f32),
        pltpu.VMEM((2, pairs) + block, f32),
        pltpu.VMEM((2, rows_n) + block, f32),
        pltpu.VMEM((2, pairs + 1) + block, f32),
        pltpu.VMEM((rows_n, cols_n, capacity, columns), f32),
        pltpu.VMEM((2, cols_n, rows_n, capacity, columns), f32),
        pltpu.VMEM((slots, 2 * columns), bf16),
        pltpu.VMEM((rows_n, cols_n, capacity, columns), f32),
        pltpu.VMEM((2, rows_n, cols_n, capacity, columns), f32),
        pltpu.VMEM((cols_n, rows_n * capacity, 2 * columns), bf16),
        pltpu.VMEM((2, elem_count, face_count, columns), f32),
        dma((rows_n, cols_n)), dma, dma, dma((rows_n,)),
        dma((3,)), dma((3,)), dma((rows_n - 1,)), dma, dma((2, rows_n - 1)), dma((2, rows_n - 1)),
        dma((pairs,)), dma((2, pairs)), dma((rows_n,)), dma((2, rows_n)), dma((pairs + 1,)), dma((2, pairs + 1)),
        dma((rows_n, cols_n - 1)), dma((2, rows_n, cols_n - 1)),
        dma((rows_n - 1,)), dma((2, rows_n - 1)),
        dma((elem_count,)), dma((2, elem_count)),
        dma, dma((2, pairs)), dma((2, pairs)), dma((pairs,)), dma((pairs,)),
    ]
    return pl.pallas_call(
        sweeps_kernel,
        out_shape=[
            jax.ShapeDtypeStruct(volume_flat.shape, f32),
            jax.ShapeDtypeStruct((cols_n,) + block, f32),
        ],
        in_specs=[anywhere] * 4 + [in_vmem] * 2 + [in_smem] + [in_vmem] * 4,
        out_specs=[in_vmem, anywhere],
        scratch_shapes=scratch,
        compiler_params=pltpu.CompilerParams(
            collective_id=0, has_side_effects=True, vmem_limit_bytes=67043328
        ),
        cost_estimate=pl.CostEstimate(flops=1000, bytes_accessed=150_000_000, transcendentals=0),
    )(boundary_start, volume_flat, kernel, elem_mats, diag, incident, *plans, face_rows)


def shards(
    boundary_start,
    volume_start,
    diag_part,
    incident,
    kernel,
    elem_mats,
    trace_owner,
    trace_slot,
    return_owner,
    return_slot,
    face_match,
):
    rows_n, cols_n = lax.axis_size("row"), lax.axis_size("col")
    devices = rows_n * cols_n
    r, c = lax.axis_index("row"), lax.axis_index("col")
    device = r * cols_n + c
    share_rows = trace_slot.shape[0] // devices
    capacity = max(2, 2 * share_rows // devices)
    elem_count, node_count, columns = volume_start.shape

    trace_blocks = trace_owner[:, 0].reshape(devices, share_rows)
    trace_slots = trace_slot.reshape(devices, share_rows)
    return_blocks = return_owner[:, 0].reshape(devices, share_rows)
    return_slots = return_slot.reshape(devices, share_rows)
    own_trace = lax.dynamic_slice_in_dim(trace_blocks, r * cols_n, cols_n, 0)
    own_return = lax.dynamic_slice_in_dim(return_blocks, c * rows_n, rows_n, 0)
    row_owners = jnp.arange(rows_n, dtype=jnp.int32) * cols_n + c
    col_owners = r * cols_n + jnp.arange(cols_n, dtype=jnp.int32)
    masks = jnp.concatenate([
        trace_blocks == device,
        (own_trace[:, None, :] == row_owners[None, :, None]).reshape(devices, share_rows),
        (own_return[:, None, :] == col_owners[None, :, None]).reshape(devices, share_rows),
        return_blocks == device,
    ])
    places = jnp.broadcast_to(jnp.arange(share_rows, dtype=jnp.int32)[None, :], (2 * devices, share_rows))
    values = jnp.concatenate([trace_slots, places, return_slots]) + 1
    earlier = jnp.triu(jnp.ones((share_rows, share_rows), jnp.bfloat16))
    ranks = jnp.dot(masks.astype(jnp.bfloat16), earlier, preferred_element_type=jnp.float32)
    ranks = jnp.where(masks, ranks, 0.0)
    wanted = jnp.arange(1, capacity + 1, dtype=jnp.int32).astype(jnp.float32)
    hits = ranks[:, None, :] == wanted[None, :, None]
    plan = jnp.sum(jnp.where(hits, values[:, None, :], 0), axis=2) - 1
    plan = plan.reshape(4, devices * capacity)
    plans = (
        jnp.maximum(plan[0], 0),
        plan[1].reshape(cols_n, 1, rows_n * capacity),
        plan[2].reshape(rows_n, 1, cols_n * capacity),
        plan[3].reshape(1, devices * capacity),
    )
    volume_final, boundary_final = sweeps(
        boundary_start, volume_start.reshape(elem_count * node_count, columns), kernel, elem_mats,
        diag_part[None, :], incident, plans, capacity, face_match[:, None, :],
    )
    return (
        boundary_final.reshape(boundary_start.shape),
        volume_final.reshape(volume_start.shape),
    )


def solution(mesh):
    placed = (
        P("row", None),
        P(("row", "col"), None, None),
        P(("row", "col")),
        P(("row", "col"), None),
        P("row", "col"),
        P(("row", "col"), None, None),
        P(),
        P(),
        P(),
        P(),
        P(("row", "col"), None),
    )
    return jax.shard_map(
        shards,
        mesh=mesh,
        in_specs=placed,
        out_specs=(P("row", None), P(("row", "col"), None, None)),
        check_vma=False,
    )
```
